32 devices in a mesh: ctx: 4 (over z), pb: 2 (over core), ga: 4 (over y, x).
Axes of the slice: x: 2, y: 2, z: 4, core: 2. Of those that a mesh axis runs over, the one named last changes fastest.
Arguments:
- queries: bfloat16 [1024, 12288], P(('ctx', 'pb'), 'ga'), may hold values from -128 to 128
- stretch_keys: bfloat16 [1024, 768], P(('ctx', 'pb'), 'ga'), may hold values from -16 to 16
- stretch_values: bfloat16 [1024, 512], P(('ctx', 'pb'), 'ga'), may hold values from -6 to 6
- prior_cache_keys: bfloat16 [16384, 768], P('ctx', 'ga'), may hold values from -16 to 16
- cache_values: bfloat16 [16384, 512], P('ctx', 'ga'), may hold values from -6 to 6
- block_lengths: int32 [4, 256], P('ctx'), may hold values from 1 to 32, 4096 in all within a row
- compress_weights: float32 [4, 32], P('ga'), may hold values from 0.1 to 1.9
- selections: int32 [16, 4, 13], P(('ctx', 'pb'), 'ga'), may hold values from 1 to 253, as said below
- gate_logits: float32 [3, 1024, 64], P(None, ('ctx', 'pb'), 'ga'), may hold values from -6 to 6
Outputs:
- attended: bfloat16 [1024, 8192], P(('ctx', 'pb'), 'ga')
The draws below stay inside these ranges and needn't reach their ends.
Inputs may be any that keep to these rules, and one draw needn't show every extreme that they name: `block_lengths`: each row belongs to one cache shard and sums to 4096; its largest entry is 32. `selections`: each row lists 13 different blocks, never the first or one of the last two blocks of a cache shard (a shard holds 64 blocks). Over the 2 rows of one device and one group at most 7 listed blocks lie in one cache shard, and for each group one cache shard holds exactly 7 of every device's listed blocks.
All inputs are finite; a program needn't handle non-finite values.
Results may differ from the reference program's by a relative error of at most 0.011.
Values may be sent and summed in bfloat16 or wider, within the bound.
No kernel may reach another device: no remote copies, remote signals or barrier semaphores. Data moves between devices by JAX's collectives and lax.ppermute only.
A program may use at most 128 MiB of HBM per device.

```python
import math
import jax
import jax.numpy as jnp
import numpy as np
from jax import lax

HQ = 64
GROUPS = 4
DK = 192
DV = 128
CTX_DEV = 4096
QB_DEV = 2
QBLK = 64
SBLK = 64
TOPSEL = 16
NFIXED = 3
WINDOW = 512
CMAX = 32
CACHE_SHARDS = 4
QSHARDS = 8
CONTEXT = 16384
STRETCH = 1024
QBLOCKS = 16
BLK_DEV = 64
NBLK = 256
NCB_DEV = 256
NCOMP = 1024
CAP = 7


def draw_queries(key, part):
    entries = jnp.clip(2.5 * jax.random.normal(jax.random.fold_in(key, 1), (STRETCH, HQ * DK), jnp.float32), -15.0, 15.0)
    return entries.astype(jnp.bfloat16)


def draw_prior_cache_keys(key, part):
    entries = jnp.clip(jax.random.normal(jax.random.fold_in(key, 2), (CONTEXT, GROUPS * DK), jnp.float32), -6.0, 6.0)
    return entries.astype(jnp.bfloat16)


def draw_stretch_keys(key, part):
    entries = jnp.clip(jax.random.normal(jax.random.fold_in(key, 3), (STRETCH, GROUPS * DK), jnp.float32), -6.0, 6.0)
    return entries.astype(jnp.bfloat16)


def draw_selections(key, part):
    listed = TOPSEL - NFIXED
    hot_shard = jax.random.randint(jax.random.fold_in(key, 11), (GROUPS,), 0, CACHE_SHARDS)

    def one_device(device_key, hot_owner):
        first_key, second_key, third_key = jax.random.split(device_key, 3)
        candidates = CACHE_SHARDS * CAP
        owners = jnp.arange(candidates, dtype=jnp.int32) // CAP
        copies = jnp.arange(candidates, dtype=jnp.int32) % CAP
        rank_draw = jax.random.permutation(first_key, candidates).astype(jnp.int32)
        priority = jnp.where(owners == hot_owner, copies - CAP, rank_draw)
        picked = jnp.argsort(priority, stable=True)[:QB_DEV * listed]
        offset_table = jax.vmap(lambda shard_key: jax.random.permutation(shard_key, BLK_DEV - 3)[:CAP])(jax.random.split(second_key, CACHE_SHARDS))
        picked_owner = owners[picked]
        block_ids = picked_owner * BLK_DEV + 1 + offset_table[picked_owner, copies[picked]].astype(jnp.int32)
        block_ids = jax.random.permutation(third_key, block_ids)
        return block_ids.reshape(QB_DEV, listed).astype(jnp.int32)
    device_keys = jax.random.split(jax.random.fold_in(key, 12), QSHARDS * GROUPS)
    owners_hot = jnp.tile(hot_shard, QSHARDS)
    drawn = jax.vmap(one_device)(device_keys, owners_hot)
    drawn = drawn.reshape(QSHARDS, GROUPS, QB_DEV, listed)
    return jnp.transpose(drawn, (0, 2, 1, 3)).reshape(QBLOCKS, GROUPS, listed)


def steps_of(key, dims, cuts, least, largest):
    gain, own = 1.0, jax.random.fold_in(key, 6)
    for axis_at, blocks in cuts:
        steps = jnp.exp(jax.random.uniform(jax.random.fold_in(own, axis_at), (blocks,), jnp.float32, least / len(cuts), largest / len(cuts)))
        gain = gain * jnp.repeat(steps, dims[axis_at] // blocks).reshape([-1 if axis == axis_at else 1 for axis in range(len(dims))])
    return gain


def profile(count, total, reach, lean):
    portions = [(1 << 20) // math.isqrt(rank ** lean) + 1 for rank in range(2, count + 1)]
    rest, holding = total - reach - (count - 1), [1] * (count - 1)
    while rest > 0:
        movable = [i for i in range(count - 1) if holding[i] < reach]
        pool, budget = sum([portions[i] for i in movable]), rest
        for i in movable:
            extra = min(reach - holding[i], max(1, budget * portions[i] // pool), rest)
            holding[i] = holding[i] + extra
            rest = rest - extra
    return np.array([reach] + holding)


def uneven_parts(rng, amount, total, limit, slope):
    if amount == 2:
        one = jax.random.randint(rng, (), max(1, total - limit), min(limit, total - 1) + 1)
        return jnp.stack([one, total - one])
    tallies = jnp.asarray(profile(amount, total, limit, slope), jnp.int32)
    twos = (amount - 1) // 2
    donor, taker = tallies[1:1 + 2 * twos:2], tallies[2:2 + 2 * twos:2]
    margin = jnp.minimum(donor - 1, limit - taker)
    shifted = jax.random.randint(jax.random.fold_in(rng, 1), (twos,), 0, 1 << 20) % (margin + 1)
    tallies = tallies.at[1:1 + 2 * twos:2].set(donor - shifted).at[2:2 + 2 * twos:2].set(taker + shifted)
    return tallies[jax.random.permutation(jax.random.fold_in(rng, 2), amount)]


def scatter_about(key, dims, scale, most, shards=(), kind=jnp.bfloat16):
    level = steps_of(key, dims, shards, -0.22, 0.18) if shards else 1.0
    values = jax.random.normal(key, dims, jnp.float32) * scale * level
    return jnp.minimum(jnp.maximum(values, -most), most).astype(kind)


def setup_inputs(seed: int = 0) -> dict:
    seeds = jax.random.split(jax.random.key(seed), 10)
    return {
        "queries": draw_queries(jax.random.fold_in(seeds[9], 71), 0),
        "stretch_keys": draw_stretch_keys(jax.random.fold_in(seeds[9], 71), 0),
        "stretch_values": scatter_about(seeds[2], (STRETCH, GROUPS * DV), 1.0, 6.0, ((0, 8), (1, 4))),
        "prior_cache_keys": draw_prior_cache_keys(jax.random.fold_in(seeds[9], 71), 0),
        "cache_values": scatter_about(seeds[4], (CONTEXT, GROUPS * DV), 1.0, 6.0, ((0, 4), (1, 4))),
        "block_lengths": jax.vmap(lambda own: uneven_parts(own, NCB_DEV, CTX_DEV, CMAX, 1))(jax.random.split(seeds[5], CACHE_SHARDS)).reshape((CACHE_SHARDS, NCB_DEV)).astype(jnp.int32),
        "compress_weights": jnp.clip(1.0 + 0.18 * jax.random.normal(seeds[6], (GROUPS, CMAX), jnp.float32), 0.1, 1.9),
        "selections": draw_selections(jax.random.fold_in(seeds[9], 71), 0),
        "gate_logits": scatter_about(seeds[8], (3, STRETCH, HQ), 1.5, 6.0, ((1, 8), (2, 4)), jnp.float32),
    }


floor_score = -1e+30

def compress_rows(cache_rows, value_rows, lengths, branch_weights):
    span = cache_rows.shape[0]
    starts = (jnp.cumsum(lengths) - lengths).astype(jnp.int32)
    positions = jnp.arange(span, dtype=jnp.int32)
    group_member = (positions[None, :] >= starts[:, None]) & (positions[None, :] < (starts + lengths)[:, None])
    offsets = lax.optimization_barrier(jnp.sum(jnp.where(group_member, positions[None, :] - starts[:, None], 0), axis=0)).astype(jnp.int32)
    lookup = jnp.arange(branch_weights.shape[0], dtype=jnp.int32)
    token_weight = lax.optimization_barrier(jnp.sum(jnp.where(offsets[:, None] == lookup[None, :], branch_weights[None, :], 0.0), axis=1))
    spread = 1.0 / jnp.sqrt(lengths.astype(jnp.float32))
    matrix = jnp.where(group_member, token_weight[None, :] * spread[:, None], 0.0).astype(jnp.bfloat16)
    packed_keys = jnp.dot(matrix.astype(jnp.float32), cache_rows.astype(jnp.float32), preferred_element_type=jnp.float32).astype(jnp.bfloat16)
    packed_values = jnp.dot(matrix.astype(jnp.float32), value_rows.astype(jnp.float32), preferred_element_type=jnp.float32).astype(jnp.bfloat16)
    return (packed_keys, packed_values)

def softmax_mix(scores, value_rows):
    row_peak = lax.optimization_barrier(jnp.max(scores, axis=1, keepdims=True))
    branch_weights = jnp.exp(scores - row_peak)
    row_total = lax.optimization_barrier(jnp.sum(branch_weights, axis=1, keepdims=True))
    return jnp.dot(branch_weights.astype(jnp.bfloat16).astype(jnp.float32), value_rows.astype(jnp.float32), preferred_element_type=jnp.float32) / row_total

def reference(queries, stretch_keys, stretch_values, prior_cache_keys, cache_values, block_lengths, compress_weights, selections, gate_logits):
    head_count = HQ // GROUPS
    score_scale = 1.0 / math.sqrt(DK)
    always_on = jnp.array([0, NBLK - 2, NBLK - 1], dtype=jnp.int32)
    near_range = jnp.arange(WINDOW + QBLK, dtype=jnp.int32)
    query_range = jnp.arange(QBLK, dtype=jnp.int32)
    results = []
    for group_index in range(GROUPS):
        group_keys = prior_cache_keys[:, group_index * DK:(group_index + 1) * DK]
        group_values = cache_values[:, group_index * DV:(group_index + 1) * DV]
        weight_row = compress_weights[group_index]
        packed_keys, packed_values = lax.map(lambda operand: compress_rows(operand[0], operand[1], operand[2], weight_row), (group_keys.reshape(CACHE_SHARDS, CTX_DEV, DK), group_values.reshape(CACHE_SHARDS, CTX_DEV, DV), block_lengths))
        packed_keys = packed_keys.reshape(NCOMP, DK)
        packed_values = packed_values.reshape(NCOMP, DV)
        key_blocks = group_keys.reshape(NBLK, SBLK, DK)
        value_blocks = group_values.reshape(NBLK, SBLK, DV)
        padded_keys = jnp.concatenate([jnp.zeros((WINDOW, DK), jnp.bfloat16), stretch_keys[:, group_index * DK:(group_index + 1) * DK]], axis=0)
        padded_values = jnp.concatenate([jnp.zeros((WINDOW, DV), jnp.bfloat16), stretch_values[:, group_index * DV:(group_index + 1) * DV]], axis=0)
        group_queries = queries[:, group_index * head_count * DK:(group_index + 1) * head_count * DK].reshape(QBLOCKS, QBLK * head_count, DK)
        group_lists = selections[:, group_index, :]

        def one_block(operand):
            query_rows, listed, block_index = operand
            compressed = softmax_mix(jnp.dot(query_rows.astype(jnp.float32), packed_keys.T.astype(jnp.float32), preferred_element_type=jnp.float32) * score_scale, packed_values)
            chosen = jnp.concatenate([always_on, listed.astype(jnp.int32)])
            selected_keys = jnp.take(key_blocks, chosen, axis=0).reshape(TOPSEL * SBLK, DK)
            chosen_values = jnp.take(value_blocks, chosen, axis=0).reshape(TOPSEL * SBLK, DV)
            selected = softmax_mix(jnp.dot(query_rows.astype(jnp.float32), selected_keys.T.astype(jnp.float32), preferred_element_type=jnp.float32) * score_scale, chosen_values)
            starting_position = (block_index * QBLK).astype(jnp.int32)
            near_keys = lax.dynamic_slice_in_dim(padded_keys, starting_position, WINDOW + QBLK, 0)
            near_values = lax.dynamic_slice_in_dim(padded_values, starting_position, WINDOW + QBLK, 0)
            key_pos = starting_position - WINDOW + near_range
            query_pos = starting_position + query_range
            distance = query_pos[:, None] - key_pos[None, :]
            allowed = (distance >= 0) & (distance < WINDOW) & (key_pos[None, :] >= 0)
            allowed = jnp.repeat(allowed, head_count, axis=0)
            near_scores = jnp.dot(query_rows.astype(jnp.float32), near_keys.T.astype(jnp.float32), preferred_element_type=jnp.float32) * score_scale
            windowed = softmax_mix(jnp.where(allowed, near_scores, floor_score), near_values)
            return (compressed, selected, windowed)
        branches = lax.map(one_block, (group_queries, group_lists, jnp.arange(QBLOCKS, dtype=jnp.int32)))
        compressed_out = branches[0].reshape(STRETCH, head_count, DV)
        selected_out = branches[1].reshape(STRETCH, head_count, DV)
        windowed_out = branches[2].reshape(STRETCH, head_count, DV)
        gate_values = jax.nn.sigmoid(gate_logits[:, :, group_index * head_count:(group_index + 1) * head_count])
        blended = gate_values[0][..., None] * compressed_out + gate_values[1][..., None] * selected_out + gate_values[2][..., None] * windowed_out
        results.append(blended.reshape(STRETCH, head_count * DV))
    return jnp.concatenate(results, axis=1).astype(jnp.bfloat16)
```

```python
import functools
import math

import jax
import jax.numpy as jnp
from jax import lax
from jax.experimental import pallas as pl
from jax.experimental.pallas import tpu as pltpu
from jax.sharding import PartitionSpec as P

SBLK = 64
WINDOW = 512
LANES = 128
FLOOR = -1e30
NFIXED = 3

VMEM = pltpu.VMEM
ANY = pl.ANY
SMEM = pltpu.SMEM


def swap(value, axis, mask):
    count = lax.axis_size(axis)
    return lax.ppermute(value, axis, [(i, i ^ mask) for i in range(count)])


def half_turn(x):
    half = x.shape[-1] // 2
    return jnp.concatenate([x[..., half:], x[..., :half]], axis=-1)


def pack_into(dst, start, keys, values):
    rows, half = keys.shape[0], keys.shape[0] // 2
    high = keys[:, LANES:]
    dst[start : start + rows, :] = keys[:, :LANES]
    dst[start + rows : start + rows + half, :] = jnp.concatenate([high[:half], high[half:]], axis=1)
    dst[start + rows + half : start + 2 * rows + half, :] = values


def unpack_from(src, start, rows, keys, values, at):
    half = rows // 2
    keys[pl.ds(at, rows), :LANES] = src[pl.ds(start, rows), :]
    high = src[pl.ds(start + rows, half), :]
    keys[pl.ds(at, half), LANES:] = high
    keys[pl.ds(at + half, half), LANES:] = half_turn(high)
    values[pl.ds(at, rows), :LANES] = src[pl.ds(start + rows + half, rows), :]


def compress_kernel(shards, per_shard, lengths, weights, keys, values, near_keys, near_values, package, packed, acc_k, acc_v):
    step, steps = pl.program_id(0), pl.num_programs(0)
    chip, core = lax.axis_index("ctx"), lax.axis_index("pb")
    span = keys.shape[0]
    blocks = lengths.shape[1]
    rows = acc_k.shape[0]
    near = near_keys.shape[0]

    lens = lengths[...].astype(jnp.float32)
    mine = lax.broadcasted_iota(jnp.int32, (rows, blocks), 0) + core * rows
    lane = lax.broadcasted_iota(jnp.int32, (rows, blocks), 1)
    starts = jnp.sum(jnp.where(lane < mine, lens, 0.0), axis=1, keepdims=True)
    own = jnp.sum(jnp.where(lane == mine, lens, 0.0), axis=1, keepdims=True)
    spread = 1.0 / jnp.sqrt(own)
    count = weights.shape[1]
    table = jnp.sum(
        jnp.where(
            lax.broadcasted_iota(jnp.int32, (count, count), 0) == lax.broadcasted_iota(jnp.int32, (count, count), 1),
            weights[...],
            0.0,
        ),
        axis=1,
        keepdims=True,
    )
    position = (lax.broadcasted_iota(jnp.int32, (1, span), 1) + step * span).astype(jnp.float32)
    ahead = position - starts
    member = (ahead >= 0) & (ahead < own)
    offset = jnp.sum(jnp.where(member, ahead, 0.0), axis=0, keepdims=True)
    lookup = lax.broadcasted_iota(jnp.int32, (count, span), 0).astype(jnp.float32)
    token = jnp.sum(jnp.where(offset == lookup, table, 0.0), axis=0, keepdims=True)
    matrix = jnp.where(member, token * spread, 0.0).astype(jnp.bfloat16)
    part_k = jnp.dot(matrix, keys[...], preferred_element_type=jnp.float32)
    part_v = jnp.dot(matrix, values[...], preferred_element_type=jnp.float32)

    @pl.when(step == 0)
    def _():
        acc_k[...] = part_k
        acc_v[...] = part_v

    @pl.when(step > 0)
    def _():
        acc_k[...] += part_k
        acc_v[...] += part_v

    for j in range(span // SBLK):
        here = slice(j * SBLK, (j + 1) * SBLK)
        pack_into(packed.at[j], 0, keys[here, :], values[here, :])

    unit = 5 * rows // 2
    near_unit = 5 * near // 2

    @pl.when(step == 0)
    def _():
        pack_into(package, unit, near_keys[...], near_values[...])
        package[unit + near_unit :, :] = packed[0]

    @pl.when(step == steps - 1)
    def _():
        pack_into(package, 0, acc_k[...].astype(jnp.bfloat16), acc_v[...].astype(jnp.bfloat16))

        @pl.when(chip == shards - 1)
        def _():
            last = span // SBLK - 2
            package[unit + near_unit :, :] = packed[last + core]


def compress(shards, cache_keys, cache_values, lengths, weights, near_keys, near_values):
    total, key_width = cache_keys.shape
    value_width = cache_values.shape[1]
    per_shard = total // SBLK
    rows = lengths.shape[1] // lax.axis_size("pb")
    near = near_keys.shape[0]
    steps = 4
    span = total // steps
    unit = 5 * SBLK // 2
    height = 5 * rows // 2 + 5 * near // 2 + unit
    whole = lambda a: pl.BlockSpec(a.shape, lambda i: (0,) * a.ndim)
    return pl.pallas_call(
        functools.partial(compress_kernel, shards, per_shard),
        grid=(steps,),
        in_specs=[
            whole(lengths),
            whole(weights),
            pl.BlockSpec((span, key_width), lambda i: (i, 0)),
            pl.BlockSpec((span, value_width), lambda i: (i, 0)),
            whole(near_keys),
            whole(near_values),
        ],
        out_specs=[
            pl.BlockSpec((height, LANES), lambda i: (0, 0)),
            pl.BlockSpec((span // SBLK, unit, LANES), lambda i: (i, 0, 0)),
        ],
        out_shape=[
            jax.ShapeDtypeStruct((height, LANES), jnp.bfloat16),
            jax.ShapeDtypeStruct((per_shard, unit, LANES), jnp.bfloat16),
        ],
        scratch_shapes=[VMEM((rows, key_width), jnp.float32), VMEM((rows, value_width), jnp.float32)],
        compiler_params=pltpu.CompilerParams(vmem_limit_bytes=24 << 20),
        cost_estimate=pl.CostEstimate(flops=2 * rows * total * 384, bytes_accessed=total * 1500, transcendentals=0),
        name="compress",
    )(lengths, weights, cache_keys, cache_values, near_keys, near_values)


def gather_kernel(count, per_shard, slots, *refs):
    lists, packed, sent, sems = refs[:count], refs[count], refs[count + 1 : 2 * count + 1], refs[-1]
    me = lax.axis_index("ctx")
    blocks, _, listed = lists[0].shape
    for x in range(count):
        dst, sem, ids = sent[x], sems.at[x], lists[x]

        def fetch(which, slot):
            pltpu.make_async_copy(packed.at[which], dst.at[slot], sem).start()

        found = jnp.int32(0)
        for b in range(blocks):
            for j in range(listed):
                wanted = ids[b, 0, j]
                here = wanted // per_shard == me

                @pl.when(here)
                def _():
                    fetch(lax.rem(wanted, per_shard), found)

                found = found + here.astype(jnp.int32)

        @pl.loop(found, slots)
        def _(slot):
            fetch(0, slot)

    for x in range(count):
        pltpu.make_async_copy(sent[x], sent[x], sems.at[x]).wait()


def gather(lists, packed, slots):
    count = len(lists)
    per_shard, unit, _ = packed.shape
    shape = jax.ShapeDtypeStruct((slots, unit, LANES), jnp.bfloat16)
    return pl.pallas_call(
        functools.partial(gather_kernel, count, per_shard, slots),
        in_specs=[pl.BlockSpec(memory_space=SMEM)] * count + [pl.BlockSpec(memory_space=ANY)],
        out_specs=[pl.BlockSpec(memory_space=VMEM)] * count,
        out_shape=[shape] * count,
        scratch_shapes=[pltpu.SemaphoreType.DMA((count,))],
        compiler_params=pltpu.CompilerParams(vmem_limit_bytes=16 << 20),
        cost_estimate=pl.CostEstimate(flops=0, bytes_accessed=2 * count * slots * unit * 256, transcendentals=0),
        name="gather",
    )(*lists, packed)


def soft(scale, query, keys, values, bias=None):
    scores = lax.dot_general(query, keys, (((1,), (1,)), ((), ())), preferred_element_type=jnp.float32)
    if bias is not None:
        rows, width = scores.shape
        scores = (scores.reshape(-1, *bias.shape) + bias[None]).reshape(rows, width)
    peak = jnp.max(scores, axis=1, keepdims=True)
    weights = jnp.exp2((scores - peak) * scale).astype(jnp.bfloat16)
    return peak, jnp.dot(weights, values, preferred_element_type=jnp.float32)


def gate_column(gate, which, rows, head):
    logits = gate[which, rows, :]
    lane = lax.broadcasted_iota(jnp.int32, logits.shape, 1)
    return jax.nn.sigmoid(jnp.sum(jnp.where(lane == head, logits, 0.0), axis=1, keepdims=True))


def near_kernel(
    shards, slots, per_shard, queries, gate, chosen, *refs
):
    packages = refs[: 2 * shards]
    base, spread_queries, fixed, where = refs[2 * shards : 2 * shards + 4]
    parts, comp_k, comp_v, near_k, near_v, bias, tally, sems = refs[2 * shards + 4 :]
    chip, core = lax.axis_index("ctx"), lax.axis_index("pb")
    cores = 2
    copies = [pltpu.make_async_copy(packages[x], parts.at[x], sems.at[x]) for x in range(2 * shards)]
    for copy in copies:
        copy.start()
    blocks, listed = chosen.shape[0], chosen.shape[2]
    query_count = queries.shape[0]
    heads = gate.shape[2]
    block_rows = query_count // blocks
    key_width = queries.shape[1] // heads
    value_width = LANES
    unit = 5 * SBLK // 2
    near = query_count
    near_unit = 5 * near // 2
    comp_rows = comp_k.shape[0] // (2 * shards)
    comp_unit = 5 * comp_rows // 2
    scale = math.log2(math.e) / math.sqrt(key_width)

    for s in range(shards):
        tally[s] = 0
    for b in range(blocks):
        for j in range(listed):
            owner = chosen[b, 0, j] // per_shard
            rank = tally[owner]
            tally[owner] = rank + 1
            where[b * listed + j] = (owner ^ chip) * slots + rank

    tail = lax.broadcasted_iota(jnp.int32, (block_rows, 2 * LANES), 1) < key_width
    for b in range(blocks):
        for h in range(heads):
            left = h * key_width // LANES * LANES
            rows = queries[b * block_rows : (b + 1) * block_rows, left : left + 2 * LANES]
            if h * key_width % LANES:
                low, mid, high = rows[:, : LANES // 2], rows[:, LANES // 2 : LANES], rows[:, LANES:]
                rows = jnp.concatenate([mid, high, low], axis=1)
            rows = jnp.where(tail, rows, jnp.zeros_like(rows))
            spread_queries[b, h * block_rows : (h + 1) * block_rows, :] = rows

    ones = jnp.ones((comp_v.shape[0], LANES), jnp.bfloat16)
    comp_v[:, LANES:] = ones
    near_v[:, LANES:] = ones[: near_v.shape[0]]
    row = lax.broadcasted_iota(jnp.int32, bias.shape[1:], 0)
    column = lax.broadcasted_iota(jnp.int32, bias.shape[1:], 1)
    device = chip * cores + core
    reach = near_k.shape[0] // near - 1
    for b in range(blocks):
        distance = row + WINDOW - column
        place = (device - reach) * near + b * block_rows + column
        allowed = (distance >= 0) & (distance < WINDOW) & (place >= 0)
        bias[b] = jnp.where(allowed, 0.0, FLOOR)

    for copy in copies:
        copy.wait()
    for x in range(2 * shards):
        unpack_from(parts.at[x], 0, comp_rows, comp_k, comp_v, x * comp_rows)
    for j in range(reach + 1):
        source = jnp.maximum(device - reach + j, 0)
        other = (source % cores != core).astype(jnp.int32)
        index = other * shards + (source // cores ^ chip)
        unpack_from(parts.at[index], comp_unit, near, near_k, near_v, j * near)
    last = shards - 1
    fixed[0] = parts[chip, comp_unit + near_unit :, :]
    for c in range(cores):
        other = (core != c).astype(jnp.int32)
        fixed[1 + c] = parts[other * shards + (last ^ chip), comp_unit + near_unit :, :]

    tile_heads = 4
    tile = tile_heads * block_rows
    chunk = min(1024, comp_k.shape[0])
    chunks = comp_k.shape[0] // chunk
    width = bias.shape[2]

    @pl.loop(0, blocks * heads // tile_heads)
    def _(t):
        b, first = t // (heads // tile_heads), lax.rem(t, heads // tile_heads) * tile_heads
        at = pl.multiple_of(first * block_rows, tile)
        query = spread_queries[b, pl.ds(at, tile), :]
        peak, total = soft(scale, query, comp_k[:chunk, :], comp_v[:chunk, :])
        if chunks > 1:

            def more(c, state):
                peak, total = state
                here = pl.ds(pl.multiple_of(c * chunk, chunk), chunk)
                new_peak, new_total = soft(scale, query, comp_k[here, :], comp_v[here, :])
                top = jnp.maximum(peak, new_peak)
                return top, total * jnp.exp2((peak - top) * scale) + new_total * jnp.exp2((new_peak - top) * scale)

            peak, total = lax.fori_loop(1, chunks, more, (peak, total))
        begin = pl.multiple_of(b * block_rows, block_rows)
        _, close = soft(scale, query, near_k[pl.ds(begin, width), :], near_v[pl.ds(begin, width), :], bias[b])
        for k in range(tile_heads):
            rows = pl.ds(begin, block_rows)
            some = slice(k * block_rows, (k + 1) * block_rows)
            far_gate = gate_column(gate, 0, rows, first + k)
            near_gate = gate_column(gate, 2, rows, first + k)
            base[b, pl.ds(pl.multiple_of(at + k * block_rows, block_rows), block_rows), :] = (
                total[some, :LANES] * (far_gate / total[some, LANES:])
                + close[some, :LANES] * (near_gate / close[some, LANES:])
            )


def near_attention(shards, slots, per_shard, queries, gate, chosen, packages):
    query_count = queries.shape[0]
    heads = gate.shape[2]
    blocks, _, listed = chosen.shape
    block_rows = query_count // blocks
    unit = 5 * SBLK // 2
    height = packages[0].shape[0]
    comp_rows = (height - unit - 5 * query_count // 2) * 2 // 5
    count = 2 * shards
    comp_total = count * comp_rows
    reach = max(1, WINDOW // query_count)
    near_total = (reach + 1) * query_count
    width = WINDOW + block_rows
    total_rows = query_count * heads
    keys = comp_total + width
    return pl.pallas_call(
        functools.partial(near_kernel, shards, slots, per_shard),
        in_specs=[pl.BlockSpec(memory_space=VMEM)] * 2
        + [pl.BlockSpec(memory_space=SMEM)]
        + [pl.BlockSpec(memory_space=ANY)] * count,
        out_specs=[pl.BlockSpec(memory_space=VMEM)] * 3 + [pl.BlockSpec(memory_space=SMEM)],
        out_shape=[
            jax.ShapeDtypeStruct((blocks, heads * block_rows, LANES), jnp.float32),
            jax.ShapeDtypeStruct((blocks, heads * block_rows, 2 * LANES), jnp.bfloat16),
            jax.ShapeDtypeStruct((NFIXED, unit, LANES), jnp.bfloat16),
            jax.ShapeDtypeStruct((blocks * listed,), jnp.int32),
        ],
        scratch_shapes=[
            VMEM((count, height, LANES), jnp.bfloat16),
            VMEM((comp_total, 2 * LANES), jnp.bfloat16),
            VMEM((comp_total, 2 * LANES), jnp.bfloat16),
            VMEM((near_total, 2 * LANES), jnp.bfloat16),
            VMEM((near_total, 2 * LANES), jnp.bfloat16),
            VMEM((blocks, block_rows, width), jnp.float32),
            SMEM((shards,), jnp.int32),
            pltpu.SemaphoreType.DMA((count,)),
        ],
        compiler_params=pltpu.CompilerParams(vmem_limit_bytes=40 << 20),
        cost_estimate=pl.CostEstimate(
            flops=4 * total_rows * keys * 256, bytes_accessed=6 << 20, transcendentals=total_rows * keys
        ),
        name="near",
    )(queries, gate, chosen, *packages)


def far_kernel(shards, where, queries, base, gate, fixed, *refs):
    pieces = refs[:shards]
    out, parts, keys, values, sems = refs[shards:]
    copies = [pltpu.make_async_copy(pieces[x], parts.at[x], sems.at[x]) for x in range(shards)]
    for copy in copies:
        copy.start()
    blocks, rows_each, _ = queries.shape
    heads = gate.shape[2]
    slots = pieces[0].shape[0]
    block_rows = rows_each // heads
    listed = where.shape[0] // blocks
    value_width = LANES
    key_width = 3 * SBLK
    scale = math.log2(math.e) / math.sqrt(key_width)
    values[:, :, LANES:] = jnp.ones((blocks, values.shape[1], LANES), jnp.bfloat16)
    for b in range(blocks):
        for f in range(NFIXED):
            unpack_from(fixed.at[f], 0, SBLK, keys.at[b], values.at[b], f * SBLK)
    for copy in copies:
        copy.wait()
    for b in range(blocks):

        @pl.loop(0, listed)
        def _(j):
            slot = where[b * listed + j]
            at = pl.multiple_of((NFIXED + j) * SBLK, SBLK)
            unpack_from(parts.at[slot // slots, lax.rem(slot, slots)], 0, SBLK, keys.at[b], values.at[b], at)

    tile_heads = 4
    tile = tile_heads * block_rows

    @pl.loop(0, blocks * heads // tile_heads)
    def _(t):
        b, first = t // (heads // tile_heads), lax.rem(t, heads // tile_heads) * tile_heads
        at = pl.multiple_of(first * block_rows, tile)
        query = queries[b, pl.ds(at, tile), :]
        _, total = soft(scale, query, keys[b], values[b])
        rows = pl.ds(pl.multiple_of(b * block_rows, block_rows), block_rows)
        for k in range(tile_heads):
            some = slice(k * block_rows, (k + 1) * block_rows)
            weight = gate_column(gate, 1, rows, first + k)
            both = base[b, pl.ds(pl.multiple_of(at + k * block_rows, block_rows), block_rows), :] + total[
                some, :LANES
            ] * (weight / total[some, LANES:])
            out[rows, pl.ds(pl.multiple_of((first + k) * LANES, LANES), LANES)] = both.astype(out.dtype)


def far_attention(shards, where, queries, base, gate, fixed, pieces):
    blocks, rows_each, _ = queries.shape
    heads = gate.shape[2]
    block_rows = rows_each // heads
    listed = where.shape[0] // blocks
    span = (NFIXED + listed) * SBLK
    slots, unit, _ = pieces[0].shape
    return pl.pallas_call(
        functools.partial(far_kernel, shards),
        in_specs=[pl.BlockSpec(memory_space=SMEM)]
        + [pl.BlockSpec(memory_space=VMEM)] * 4
        + [pl.BlockSpec(memory_space=ANY)] * shards,
        out_specs=pl.BlockSpec(memory_space=VMEM),
        out_shape=jax.ShapeDtypeStruct((blocks * block_rows, heads * LANES), jnp.bfloat16),
        scratch_shapes=[
            VMEM((shards, slots, unit, LANES), jnp.bfloat16),
            VMEM((blocks, span, 2 * LANES), jnp.bfloat16),
            VMEM((blocks, span, 2 * LANES), jnp.bfloat16),
            pltpu.SemaphoreType.DMA((shards,)),
        ],
        compiler_params=pltpu.CompilerParams(vmem_limit_bytes=40 << 20),
        cost_estimate=pl.CostEstimate(
            flops=4 * blocks * rows_each * span * 256, bytes_accessed=4 << 20, transcendentals=blocks * rows_each * span
        ),
        name="far",
    )(where, queries, base, gate, fixed, *pieces)


def on_device(
    queries,
    stretch_keys,
    stretch_values,
    prior_cache_keys,
    cache_values,
    block_lengths,
    compress_weights,
    selections,
    gate_logits,
):
    shards = lax.axis_size("ctx")
    per_shard = prior_cache_keys.shape[0] // SBLK
    blocks, _, listed = selections.shape
    slots = max(2, (blocks * listed + shards - 1) // shards)

    lists = [selections] + [swap(selections, "ctx", x) for x in range(1, shards)]
    package, packed = compress(
        shards, prior_cache_keys, cache_values, block_lengths, compress_weights, stretch_keys, stretch_values
    )
    gathered = {0: package}
    bit = shards // 2
    while bit:
        gathered.update({x | bit: swap(value, "ctx", bit) for x, value in list(gathered.items())})
        bit //= 2
    packages = [gathered[x] for x in range(shards)]
    packages = packages + [swap(value, "pb", 1) for value in packages]
    sent = gather(lists, packed, slots)
    pieces = [sent[0]] + [swap(sent[x], "ctx", x) for x in range(1, shards)]
    base, spread_queries, fixed, where = near_attention(
        shards, slots, per_shard, queries, gate_logits, selections, packages
    )
    return far_attention(shards, where, spread_queries, base, gate_logits, fixed, pieces)


def solution(mesh):
    placed = (
        P(("ctx", "pb"), "ga"),
        P(("ctx", "pb"), "ga"),
        P(("ctx", "pb"), "ga"),
        P("ctx", "ga"),
        P("ctx", "ga"),
        P("ctx", None),
        P("ga", None),
        P(("ctx", "pb"), "ga", None),
        P(None, ("ctx", "pb"), "ga"),
    )
    return jax.shard_map(
        on_device, mesh=mesh, in_specs=placed, out_specs=P(("ctx", "pb"), "ga"), check_vma=False
    )
```
